32 devices in a mesh: copy: 2 (over y), grid: 4 (over z), blk: 2 (over x), sub: 2 (over core).
Axes of the slice: x: 2, y: 2, z: 4, core: 2. Of those that a mesh axis runs over, the one named last changes fastest.
Arguments:
- ensemble: float32 [128, 3, 256, 1024], P(('copy', 'grid'), None, 'blk', 'sub'), parts along dimension 0, may hold values from -6 to 6
- basin_thickness: float32 [512, 1024], P(('copy', 'blk'), 'sub'), parts along dimension 0, may hold values from 0.25 to 2
- wet_indicator: int32 [512, 1024], P(('copy', 'blk'), 'sub'), parts along dimension 0, may hold values 0 or 1
- obs_cell: int32 [4, 4, 2, 64], P(('copy', 'blk'), 'grid', 'sub'), parts along dimension 0, may hold values from 0 to 16383
- obs_count: int32 [4, 4, 2], P(('copy', 'blk'), 'grid', 'sub'), parts along dimension 0, may hold values from 16 to 64, as said below
- obs_value: float32 [4, 4, 2, 64], P(('copy', 'blk'), 'grid', 'sub'), parts along dimension 0, may hold values from -6 to 6
- obs_error: float32 [4, 4, 2, 64], P(('copy', 'blk'), 'grid', 'sub'), parts along dimension 0, may hold values from 0.5 to 2
Outputs:
- analysis: float32 [128, 3, 2, 128, 1024], P('copy', None, 'blk', 'grid', 'sub'), parts along dimension 0
The draws below stay inside these ranges and needn't reach their ends.
There are 2 independent parts, one for each index of `copy`. The reference program is written for one: setup_inputs(seed, part) draws one part's arguments, and reference() takes and returns one part's arrays. A program takes and returns all parts, laid end to end along the dimension named above; each array names one. Nothing has to cross between parts.
Inputs may be any that keep to these rules, and one draw needn't show every extreme that they name: `obs_count`: one block of every draw has all 64 slots live.
All inputs are finite; a program needn't handle non-finite values. No bound on the sum of `wet_indicator` on one device may be relied on, other than what follows from the above.
Results may differ from the reference program's by a relative error of at most 0.0003.
Values sent between devices are 32-bit elements; how exact they have to be, the bound alone decides.
No kernel may reach another device: no remote copies, remote signals or barrier semaphores. Data moves between devices by JAX's collectives and lax.ppermute only.
A program may use at most 128 MiB of HBM per device.

```python
import math
import jax
import jax.numpy as jnp
from jax import lax

K = 64
CX = 128
CY = 512
OBS = 64
STEPS = 2
NS_STEPS = 8
RB = 32
NX = 256
NY = 1024
N_GRID = 4
N_BLK = 2
N_SUB = 2


def draw_obs_count(key, part):
    shape = (N_BLK, N_GRID, N_SUB)
    lowest = max(1, OBS // 4)
    counts = jax.random.randint(key, shape, lowest, OBS + 1, dtype=jnp.int32).reshape(-1)
    chosen = jax.random.randint(jax.random.fold_in(key, 7), (), 0, counts.shape[0], dtype=jnp.int32)
    counts = jnp.where(jnp.arange(counts.shape[0], dtype=jnp.int32) == chosen, OBS, counts)
    return counts.reshape(shape).astype(jnp.int32)


def plant(values, key, least, top_value):
    longest = values.shape.index(max(values.shape))
    spots = []
    for shift in (0, 1):
        where = [jax.random.randint(jax.random.fold_in(key, axis), (), 0, length) for axis, length in enumerate(values.shape)]
        where[longest] = (where[longest] + shift) % values.shape[longest]
        spots.append(tuple(where))
    return values.at[spots[0]].set(least).at[spots[1]].set(top_value)


def levels(own_key, dims, pieces, least, largest):
    level = 1.0
    for position, shards_of in pieces:
        steps = jax.random.uniform(jax.random.fold_in(jax.random.fold_in(own_key, 6), position), (shards_of,), jnp.float32, least / len(pieces), largest / len(pieces))
        level = level * jnp.repeat(jnp.exp(steps), dims[position] // shards_of).reshape((-1,) + (1,) * (len(dims) - 1 - position))
    return level


def noise(rng, dims, scale, limit, shards=(), kind=jnp.bfloat16):
    values = jax.random.normal(rng, dims, jnp.float32) * scale
    if len(shards) > 0:
        values = levels(rng, dims, shards, -0.22, 0.18) * values
    return jnp.clip(values, min=-limit, max=limit).astype(kind)


def setup_inputs(seed: int = 0, part: int = 0) -> dict:
    key_of = jax.random.split(jax.random.key(seed), 8)
    own_keys = jax.random.split(jax.random.fold_in(key_of[7], part), 8)
    return {
        "ensemble": noise(own_keys[0], (K, 3, NX, NY), 1.0, 6.0, ((0, 4), (2, 2), (3, 2)), jnp.float32),
        "basin_thickness": jnp.clip(jnp.exp(math.log(2.0) - 2.0794415 * jax.random.uniform(own_keys[1], (NX, NY), jnp.float32) ** levels(own_keys[1], (NX, NY), ((0, 2), (1, 2)), -0.2, 0.2)), 0.25, 2.0),
        "wet_indicator": plant((jax.random.randint(own_keys[2], (NX, NY), 0, 5) < 4).astype(jnp.int32), jax.random.fold_in(own_keys[2], 1), 0, 1),
        "obs_cell": plant(jax.random.randint(own_keys[3], (N_BLK, N_GRID, N_SUB, OBS), 0, RB * CY), jax.random.fold_in(own_keys[3], 1), 0, (RB * CY) - 1).astype(jnp.int32),
        "obs_count": draw_obs_count(jax.random.fold_in(jax.random.fold_in(key_of[7], part), 71), part),
        "obs_value": noise(own_keys[5], (N_BLK, N_GRID, N_SUB, OBS), 1.5, 6.0, ((0, 2), (1, 4), (2, 2)), jnp.float32),
        "obs_error": jnp.clip(jnp.exp(math.log(2.0) - 1.3862944 * jax.random.uniform(own_keys[6], (N_BLK, N_GRID, N_SUB, OBS), jnp.float32) ** levels(own_keys[6], (N_BLK, N_GRID, N_SUB, OBS), ((0, 2), (1, 4), (2, 2)), -0.2, 0.2)), 0.5, 2.0),
    }


FRICTION = 0.05
PRESSURE = 0.35
DIVERGE = 0.35
CORIOLIS = 0.2
precise = lax.Precision.HIGHEST

def along_first(field):
    bordered_array = jnp.pad(field, [(0, 0)] * (field.ndim - 2) + [(1, 1), (0, 0)])
    return bordered_array[..., 2:, :] - bordered_array[..., :-2, :]

def along_second(field):
    bordered_array = jnp.pad(field, [(0, 0)] * (field.ndim - 1) + [(1, 1)])
    return bordered_array[..., 2:] - bordered_array[..., :-2]

def propagate_prior(dynamic_vector, basin_thickness, shore_indicator, latitude_coupling):
    height = dynamic_vector[:, 0]
    first = dynamic_vector[:, 1]
    second = dynamic_vector[:, 2]
    first_new = shore_indicator * ((1.0 - FRICTION) * first + latitude_coupling * second - PRESSURE * along_first(height))
    second_new = shore_indicator * ((1.0 - FRICTION) * second - latitude_coupling * first - PRESSURE * along_second(height))
    height_new = height - DIVERGE * (along_first(basin_thickness * first_new) + along_second(basin_thickness * second_new))
    return jnp.stack([height_new, first_new, second_new], axis=1)

def transform(gram, proj):
    eye = jnp.eye(K, dtype=jnp.float32)
    system = eye + gram
    mean_w = jnp.linalg.solve(system, proj)
    scale = jnp.sqrt(jnp.sum(system * system))
    ystate = system / scale
    zstate = eye
    for sweep in range(NS_STEPS):
        factor = 1.5 * eye - 0.5 * jnp.dot(zstate, ystate, precision=precise)
        ystate = jnp.dot(ystate, factor, precision=precise)
        zstate = jnp.dot(factor, zstate, precision=precise)
    return mean_w[:, None] + zstate / jnp.sqrt(scale)

def reference(ensemble, basin_thickness, wet_indicator, obs_cell, obs_count, obs_value, obs_error):
    shore_indicator = wet_indicator.astype(jnp.float32)
    rows = jnp.arange(NX, dtype=jnp.float32)
    latitude_coupling = (CORIOLIS * (2.0 * (rows + 0.5) / NX - 1.0))[:, None]
    dynamic_vector = ensemble
    for number in range(STEPS):
        dynamic_vector = propagate_prior(dynamic_vector, basin_thickness, shore_indicator, latitude_coupling)
    split = dynamic_vector.reshape(K, 3, N_BLK, N_GRID, RB, NY)

    def domain(index):
        index = index.astype(jnp.int32)
        local = lax.dynamic_index_in_dim(split, index, 3, keepdims=False)
        cells = lax.dynamic_index_in_dim(obs_cell, index, 1, keepdims=False)
        counts = lax.dynamic_index_in_dim(obs_count, index, 1, keepdims=False)
        values = lax.dynamic_index_in_dim(obs_value, index, 1, keepdims=False)
        errors = lax.dynamic_index_in_dim(obs_error, index, 1, keepdims=False)
        surface_height = local[:, 0].reshape(K, N_BLK, RB, N_SUB, CY).transpose(0, 1, 3, 2, 4).reshape(K, N_BLK, N_SUB, RB * CY)
        picked = jnp.take_along_axis(surface_height, jnp.broadcast_to(cells[None], (K,) + cells.shape), axis=3).reshape(K, -1)
        pbar = lax.optimization_barrier(jnp.mean(picked, axis=0))
        valid = (jnp.arange(OBS, dtype=jnp.int32)[None, None, :] < counts[:, :, None]).reshape(-1)
        scale = jnp.where(valid, 1.0 / (errors.reshape(-1) * math.sqrt(K - 1)), 0.0)
        anomobs = (picked - pbar) * scale
        innov = (values.reshape(-1) - pbar) * scale
        gram = jnp.dot(anomobs, anomobs.T, precision=precise)
        proj = jnp.dot(anomobs, innov, precision=precise)
        weights = transform(gram, proj)
        flat = local.reshape(K, -1)
        center = lax.optimization_barrier(jnp.mean(flat, axis=0))
        member_deviations = flat - center
        return (center + jnp.dot(weights.T, member_deviations, precision=precise)).reshape(K, 3, N_BLK, RB, NY)
    results = lax.map(domain, jnp.arange(N_GRID, dtype=jnp.int32))
    return results.transpose(1, 2, 3, 0, 4, 5).reshape(K, 3, N_BLK, CX, NY)
```

```python
import math

import jax
import jax.numpy as jnp
from jax import lax
from jax.experimental import pallas as pl
from jax.experimental.pallas import tpu as pltpu
from jax.sharding import PartitionSpec as P

STEPS = 2
NS_STEPS = 8
HALO = 4
LANES = 128

FRICTION = 0.05
PRESSURE = 0.35
DIVERGE = 0.35
CORIOLIS = 0.2
precise = lax.Precision.HIGHEST


def neighbours(head, tail, axis):
    count = lax.axis_size(axis)
    if count == 2:
        index = lax.axis_index(axis)
        got = lax.ppermute(jnp.where(index == 0, tail, head), axis, [(0, 1), (1, 0)])
        zero = jnp.zeros_like(got)
        return jnp.where(index == 1, got, zero), jnp.where(index == 0, got, zero)
    before = lax.ppermute(tail, axis, [(i, i + 1) for i in range(count - 1)])
    after = lax.ppermute(head, axis, [(i + 1, i) for i in range(count - 1)])
    return before, after


def forecast_kernel(x_ref, rows_ref, cols_ref, depth_ref, wet_ref, inside_ref, cor_ref, h_ref, u_ref, v_ref):
    core_rows, core_cols = x_ref.shape[2], x_ref.shape[3]
    rows = core_rows + 2 * HALO
    cols = core_cols + LANES

    def full(field):
        tall = jnp.concatenate([x_ref[0, field], rows_ref[0, field]], axis=0)
        return jnp.concatenate([tall, cols_ref[0, field]], axis=1)

    def along_first(q):
        return pltpu.roll(q, rows - 1, 0) - pltpu.roll(q, 1, 0)

    def along_second(q):
        return pltpu.roll(q, cols - 1, 1) - pltpu.roll(q, 1, 1)

    h, u, v = full(0), full(1), full(2)
    wet = wet_ref[...]
    depth = depth_ref[...]
    inside = inside_ref[...]
    cor = jnp.broadcast_to(cor_ref[:, :1], (rows, cols))
    for number in range(STEPS):
        first = wet * ((1.0 - FRICTION) * u + cor * v - PRESSURE * along_first(h))
        second = wet * ((1.0 - FRICTION) * v - cor * u - PRESSURE * along_second(h))
        h = inside * (h - DIVERGE * (along_first(depth * first) + along_second(depth * second)))
        u, v = first, second
    for ref, value in ((h_ref, h), (u_ref, u), (v_ref, v)):
        ref[:, 0] = value[:core_rows, :core_cols].reshape(ref.shape[0], ref.shape[2], core_cols)


def forecast(ensemble, basin_thickness, wet_indicator):
    members, fields, core_rows, core_cols = ensemble.shape
    parts = lax.axis_size("grid")
    static = jnp.stack([basin_thickness, wet_indicator.astype(jnp.float32)])
    flat = ensemble.reshape(members * fields, core_rows, core_cols)

    def edge(lo, hi):
        return jnp.concatenate([flat[:, lo:hi], static[:, lo:hi]], axis=0)

    before, after = neighbours(edge(0, HALO), edge(core_rows - HALO, core_rows), "blk")
    row_halo = jnp.concatenate([after, before], axis=1)

    def side(lo, hi):
        core = jnp.concatenate([flat[:, :, lo:hi], static[:, :, lo:hi]], axis=0)
        return jnp.concatenate([core, row_halo[:, :, lo:hi]], axis=1)

    before, after = neighbours(side(0, HALO), side(core_cols - HALO, core_cols), "sub")
    gap = jnp.zeros(before.shape[:2] + (LANES - 2 * HALO,), jnp.float32)
    col_halo = jnp.concatenate([after, gap, before], axis=2)
    count = members * fields

    def whole(which):
        tall = jnp.concatenate([static[which], row_halo[count + which]], axis=0)
        return jnp.concatenate([tall, col_halo[count + which]], axis=1)

    depth, wet = whole(0), whole(1)
    rows, cols = depth.shape

    def offset(size, total):
        place = jnp.arange(total, dtype=jnp.int32)
        return jnp.where(place >= total - HALO, place - total, place)

    def within(axis, size, total):
        place = offset(size, total)
        index, ends = lax.axis_index(axis), lax.axis_size(axis) - 1
        middle = (place >= 0) & (place < size)
        past = (place >= size) & (place < size + HALO) & (index < ends)
        return middle | past | ((place < 0) & (index > 0))

    inside = (within("blk", core_rows, rows)[:, None] & within("sub", core_cols, cols)[None, :]).astype(jnp.float32)
    total_rows = core_rows * lax.axis_size("blk")
    line = (lax.axis_index("blk") * core_rows + offset(core_rows, rows)).astype(jnp.float32)
    cor = CORIOLIS * (2.0 * (line + 0.5) / total_rows - 1.0)
    cor = jnp.broadcast_to(cor[:, None], (rows, LANES))
    lines = core_rows // parts

    def fixed(shape):
        return pl.BlockSpec(shape, lambda m: (0,) * len(shape))

    shape = jax.ShapeDtypeStruct((parts, members, lines, core_cols), jnp.float32)
    spec = pl.BlockSpec((parts, 1, lines, core_cols), lambda m: (0, m, 0, 0))
    return pl.pallas_call(
        forecast_kernel,
        grid=(members,),
        in_specs=[
            pl.BlockSpec((1, fields, core_rows, core_cols), lambda m: (m, 0, 0, 0)),
            pl.BlockSpec((1, fields, 2 * HALO, core_cols), lambda m: (m, 0, 0, 0)),
            pl.BlockSpec((1, fields, rows, LANES), lambda m: (m, 0, 0, 0)),
            fixed((rows, cols)),
            fixed((rows, cols)),
            fixed((rows, cols)),
            fixed((rows, LANES)),
        ],
        out_specs=[spec] * 3,
        out_shape=[shape] * 3,
        compiler_params=pltpu.CompilerParams(dimension_semantics=("arbitrary",)),
        name="forecast",
    )(
        ensemble,
        row_halo[:count].reshape(members, fields, 2 * HALO, core_cols),
        col_halo[:count].reshape(members, fields, rows, LANES),
        depth,
        wet,
        inside,
        cor,
    )


def observe(surface_height, obs_cell, obs_count, obs_value, obs_error):
    members = surface_height.shape[0]
    flat = surface_height.reshape(members, -1)
    cells = obs_cell.reshape(-1)
    picked = jnp.take(flat, cells, axis=1)
    pbar = jnp.mean(picked, axis=0)
    valid = jnp.arange(cells.shape[0], dtype=jnp.int32) < obs_count.reshape(())
    scale = jnp.where(valid, 1.0 / (obs_error.reshape(-1) * math.sqrt(members - 1)), 0.0)
    anomobs = (picked - pbar) * scale
    innov = (obs_value.reshape(-1) - pbar) * scale
    gram = jnp.dot(anomobs, anomobs.T, precision=precise)
    proj = jnp.dot(anomobs, innov, precision=precise)
    return jnp.concatenate([gram, proj[None]], axis=0)


def domain_reduction(packed):
    for axis in ("sub", "blk"):
        if lax.axis_size(axis) == 2:
            packed = packed + lax.ppermute(packed, axis, [(0, 1), (1, 0)])
        else:
            packed = lax.psum(packed, axis)
    return packed


def transform(packed):
    members = packed.shape[1]
    eye = jnp.eye(members, dtype=jnp.float32)
    system = eye + packed[:members]
    proj = packed[members]
    factor_low = jnp.linalg.cholesky(system)
    mean_w = jax.scipy.linalg.cho_solve((factor_low, True), proj)
    scale = jnp.sqrt(jnp.sum(system * system))
    ystate = system / scale
    zstate = eye
    for sweep in range(NS_STEPS):
        factor = 1.5 * eye - 0.5 * jnp.dot(zstate, ystate, precision=precise)
        ystate = jnp.dot(ystate, factor, precision=precise)
        zstate = jnp.dot(factor, zstate, precision=precise)
    return mean_w[:, None] + zstate / jnp.sqrt(scale)


def shards(ensemble, basin_thickness, wet_indicator, obs_cell, obs_count, obs_value, obs_error):
    pieces = forecast(ensemble, basin_thickness, wet_indicator)
    blocks = []
    for piece in pieces:
        got = lax.all_to_all(piece, "grid", split_axis=0, concat_axis=0, tiled=True)
        blocks.append(got.reshape((-1,) + got.shape[2:]))
    packed = domain_reduction(observe(blocks[0], obs_cell, obs_count, obs_value, obs_error))
    weights = transform(packed)
    members = weights.shape[0]
    mixing = weights - jnp.mean(weights, axis=0) + 1.0 / members
    updated = [
        lax.dot_general(mixing, block, (((0,), (0,)), ((), ())), precision=lax.Precision.HIGH)
        for block in blocks
    ]
    return jnp.stack(updated, axis=1)[:, :, None]


def solution(mesh):
    placed = (
        P(("copy", "grid"), None, "blk", "sub"),
        P(("copy", "blk"), "sub"),
        P(("copy", "blk"), "sub"),
        P(("copy", "blk"), "grid", "sub", None),
        P(("copy", "blk"), "grid", "sub"),
        P(("copy", "blk"), "grid", "sub", None),
        P(("copy", "blk"), "grid", "sub", None),
    )
    return jax.shard_map(
        shards,
        mesh=mesh,
        in_specs=placed,
        out_specs=P("copy", None, "blk", "grid", "sub"),
        check_vma=False,
    )
```
